32 devices in a mesh: groups: 2 (over y), tile: 16 (over z, x, core).
Axes of the slice: x: 2, y: 2, z: 4, core: 2. Of those that a mesh axis runs over, the one named last changes fastest.
Arguments:
- coarse: bfloat16 [12, 512, 512], P(None, ('groups', 'tile')), parts along dimension 1, may hold values from -6 to 6
- noise_field: bfloat16 [2, 12, 512, 512], P(None, None, ('groups', 'tile')), parts along dimension 2, may hold values from -6 to 6
- anchors: int32 [32, 2], P(('groups', 'tile')), parts along dimension 0, may hold values from 0 to 288
- counts: int32 [32], P(('groups', 'tile')), parts along dimension 0, may hold values from 1 to 2, as said below
- blend_weights: int32 [224, 224], replicated, may hold values from 1 to 16
- regress_lift: bfloat16 [12, 128], replicated, may hold values from -1.75 to 1.75
- regress_conv: bfloat16 [2, 9, 128, 128], replicated, may hold values from -0.1875 to 0.1875
- regress_head: bfloat16 [128, 12], replicated, may hold values from -0.5 to 0.5
- denoise_lift: bfloat16 [36, 128], replicated, may hold values from -1 to 1
- denoise_conv: bfloat16 [2, 9, 128, 128], replicated, may hold values from -0.1875 to 0.1875
- denoise_head: bfloat16 [128, 12], replicated, may hold values from -0.5 to 0.5
Outputs:
- ens_mean: float32 [12, 512, 512], P(None, ('groups', 'tile')), parts along dimension 1
- ens_var: float32 [12, 512, 512], P(None, ('groups', 'tile')), parts along dimension 1
The draws below stay inside these ranges and needn't reach their ends.
There are 2 independent parts, one for each index of `groups`. The reference program is written for one: setup_inputs(seed, part) draws one part's arguments, and reference() takes and returns one part's arrays. A program takes and returns all parts, laid end to end along the dimension named above; an argument that names none is the same for every part. Nothing has to cross between parts.
Inputs may be any that keep to these rules, and one draw needn't show every extreme that they name: The first counts[s] slots of strip s are live; some strip has all 2 live in every draw.
All inputs are finite; a program needn't handle non-finite values.
Results may differ from the reference program's by a relative error of at most 0.0034.
Values may be sent and summed in bfloat16 or wider, within the bound.
A program may use at most 320 MiB of HBM per device.

```python
import math
import jax
import jax.numpy as jnp
from jax import lax

CH = 12
WIDTH = 128
STRIP = 16
COLS = 512
PATCH = 224
POOL = 4
SLOTS = 2
MEMBERS = 2
REG_LAYERS = 2
DEN_LAYERS = 2
WEIGHT_LEVELS = 16
ROWS = 256
N_TILE = 16


def draw_counts(key, part):
    key_low, key_heavy, key_pick = jax.random.split(key, 3)
    low_counts = jax.random.randint(key_low, (N_TILE,), 1, 3)
    heavy_flag = jax.random.randint(key_heavy, (N_TILE,), 0, 4) == 0
    drawn = jnp.where(heavy_flag, SLOTS, jnp.minimum(low_counts, SLOTS))
    picked = jax.random.randint(key_pick, (), 0, N_TILE)
    drawn = drawn.at[picked].set(SLOTS)
    return drawn.astype(jnp.int32)


def plant(array, rng, low, high):
    longest = array.shape.index(max(array.shape))
    spots = []
    for shift in (0, 1):
        where = [jax.random.randint(jax.random.fold_in(rng, axis), (), 0, length) for axis, length in enumerate(array.shape)]
        where[longest] = (where[longest] + shift) % array.shape[longest]
        spots.append(tuple(where))
    return array.at[spots[0]].set(low).at[spots[1]].set(high)


def level_of(key, extent, cuts, least, largest):
    gain = 1.0
    for axis_at, shards_of in cuts:
        steps = jax.random.uniform(jax.random.fold_in(jax.random.fold_in(key, 6), axis_at), (shards_of,), jnp.float32, least / len(cuts), largest / len(cuts))
        gain = gain * jnp.repeat(jnp.exp(steps), extent[axis_at] // shards_of).reshape((-1,) + (1,) * (len(extent) - 1 - axis_at))
    return gain


def scatter_about(rng, dims, spread, bound, cuts=(), kind=jnp.bfloat16):
    loudness = level_of(rng, dims, cuts, -0.22, 0.18) if cuts else 1.0
    values = jax.random.normal(rng, dims, jnp.float32) * spread * loudness
    return jnp.minimum(jnp.maximum(values, -bound), bound).astype(kind)


def setup_inputs(seed: int = 0, part: int = 0) -> dict:
    streams_of = jax.random.split(jax.random.key(seed), 12)
    part_splits = jax.random.split(jax.random.fold_in(streams_of[11], part), 12)
    return {
        "coarse": scatter_about(part_splits[0], (CH, ROWS, COLS), 1.0, 6.0, ((1, 16),)),
        "noise_field": scatter_about(part_splits[1], (MEMBERS, CH, ROWS, COLS), 1.0, 6.0, ((2, 16),)),
        "anchors": plant(jax.random.randint(part_splits[2], (N_TILE, SLOTS), 0, COLS - PATCH + 1), jax.random.fold_in(part_splits[2], 1), 0, COLS - PATCH).astype(jnp.int32),
        "counts": draw_counts(jax.random.fold_in(jax.random.fold_in(streams_of[11], part), 71), part),
        "blend_weights": plant(jax.random.randint(streams_of[4], (PATCH, PATCH), 1, WEIGHT_LEVELS + 1), jax.random.fold_in(streams_of[4], 1), 1, WEIGHT_LEVELS).astype(jnp.int32),
        "regress_lift": scatter_about(streams_of[5], (CH, WIDTH), CH ** -0.5, 1.75),
        "regress_conv": scatter_about(streams_of[6], (REG_LAYERS, 9, WIDTH, WIDTH), (9 * WIDTH) ** -0.5, 0.1875),
        "regress_head": scatter_about(streams_of[7], (WIDTH, CH), WIDTH ** -0.5, 0.5),
        "denoise_lift": scatter_about(streams_of[8], (3 * CH, WIDTH), (3 * CH) ** -0.5, 1.0),
        "denoise_conv": scatter_about(streams_of[9], (DEN_LAYERS, 9, WIDTH, WIDTH), (9 * WIDTH) ** -0.5, 0.1875),
        "denoise_head": scatter_about(streams_of[10], (WIDTH, CH), WIDTH ** -0.5, 0.5),
    }


skip_gain = 0.2
out_gain = 0.5 / math.sqrt(1.25)
in_gain = 1.0 / math.sqrt(1.25)

def block_mean(field):
    lead = field.shape[:-2]
    row_count = field.shape[-2] // POOL
    col_count = field.shape[-1] // POOL
    grouped = field.astype(jnp.float32).reshape(lead + (row_count, POOL, col_count, POOL))
    return lax.optimization_barrier(jnp.mean(grouped, axis=(-3, -1)))

def spread_blocks(field):
    lead = field.shape[:-2]
    row_count = field.shape[-2]
    col_count = field.shape[-1]
    wide = jnp.broadcast_to(field[..., :, None, :, None], lead + (row_count, POOL, col_count, POOL))
    return wide.reshape(lead + (row_count * POOL, col_count * POOL))

def conv_cells(padded, kernel):
    row_count = padded.shape[1] - 2
    col_count = padded.shape[2] - 2
    feat_count = padded.shape[3]
    flat_kernel = kernel.reshape(9 * feat_count, kernel.shape[2])

    def conv_item(item):
        taps = [item[shift_row:shift_row + row_count, shift_col:shift_col + col_count, :] for shift_row in range(3) for shift_col in range(3)]
        stacked = jnp.concatenate(taps, axis=-1).reshape(-1, 9 * feat_count)
        return jnp.dot(stacked, flat_kernel, preferred_element_type=jnp.float32).reshape(row_count, col_count, kernel.shape[2])
    return lax.map(conv_item, padded)

def conv_same(hidden_act, kernel):
    padded = jnp.pad(hidden_act, ((0, 0), (1, 1), (1, 1), (0, 0)))
    return conv_cells(padded, kernel)

def residual_layer(hidden_act, conv_term):
    return (hidden_act.astype(jnp.float32) + jax.nn.silu(conv_term)).astype(jnp.bfloat16)

def denoise(noise_patch, cond_patch, denoise_lift, denoise_conv, denoise_head):
    channel_count = noise_patch.shape[2]
    noise_low = block_mean(noise_patch).astype(jnp.bfloat16)
    cond_low = block_mean(cond_patch).astype(jnp.bfloat16)
    lifted = in_gain * jnp.einsum('bmcij,ck->bmijk', noise_low.astype(jnp.float32), denoise_lift[:channel_count].astype(jnp.float32))
    lifted = lifted + jnp.einsum('bcij,ck->bijk', cond_low.astype(jnp.float32), denoise_lift[channel_count:].astype(jnp.float32))[:, None]
    hidden_act = lifted.astype(jnp.bfloat16)
    act_shape = hidden_act.shape
    flat_act = hidden_act.reshape((-1,) + act_shape[2:])
    for layer_index in range(denoise_conv.shape[0]):
        flat_act = residual_layer(flat_act, conv_same(flat_act, denoise_conv[layer_index]))
    head_term = jnp.einsum('nijk,kc->ncij', flat_act.astype(jnp.float32), denoise_head.astype(jnp.float32))
    head_term = head_term.reshape(act_shape[0], act_shape[1], channel_count, act_shape[2], act_shape[3])
    return skip_gain * noise_patch.astype(jnp.float32) + out_gain * spread_blocks(head_term)

def reference(coarse, noise_field, anchors, counts, blend_weights, regress_lift, regress_conv, regress_head, denoise_lift, denoise_conv, denoise_head):
    coarse_low = block_mean(coarse).astype(jnp.bfloat16)
    hidden_act = jnp.einsum('crw,ck->rwk', coarse_low.astype(jnp.float32), regress_lift.astype(jnp.float32))[None].astype(jnp.bfloat16)
    for layer_index in range(regress_conv.shape[0]):
        hidden_act = residual_layer(hidden_act, conv_same(hidden_act, regress_conv[layer_index]))
    reg_low = jnp.einsum('rwk,kc->crw', hidden_act[0].astype(jnp.float32), regress_head.astype(jnp.float32))
    reg_mean = coarse.astype(jnp.float32) + spread_blocks(reg_low)
    condition = jnp.concatenate([reg_mean.astype(jnp.bfloat16), coarse], axis=0)
    noise_pad = jnp.pad(noise_field, ((0, 0), (0, 0), (0, PATCH), (0, 0)))
    cond_pad = jnp.pad(condition, ((0, 0), (0, PATCH), (0, 0)))
    weight_tile = blend_weights.astype(jnp.float32)

    def holder_step(carried, holder_index):
        numer_all, denom_all = carried
        row_start = (holder_index * STRIP).astype(jnp.int32)
        noise_win = lax.dynamic_slice_in_dim(noise_pad, row_start, PATCH, 2)
        cond_win = lax.dynamic_slice_in_dim(cond_pad, row_start, PATCH, 1)
        numer_win = lax.dynamic_slice_in_dim(numer_all, row_start, PATCH, 2)
        denom_win = lax.dynamic_slice_in_dim(denom_all, row_start, PATCH, 0)
        for slot_index in range(SLOTS):
            column = anchors[holder_index, slot_index].astype(jnp.int32)
            live_flag = slot_index < counts[holder_index]

            def compute_patch(unused_arg):
                noise_patch = lax.dynamic_slice_in_dim(noise_win, column, PATCH, 3)[None]
                cond_patch = lax.dynamic_slice_in_dim(cond_win, column, PATCH, 2)[None]
                return denoise(noise_patch, cond_patch, denoise_lift, denoise_conv, denoise_head)[0]

            def zero_patch(unused_arg):
                return jnp.zeros((MEMBERS, CH, PATCH, PATCH), jnp.float32)
            result = lax.cond(live_flag, compute_patch, zero_patch, 0)
            weight = weight_tile * live_flag.astype(jnp.float32)
            previous = lax.dynamic_slice_in_dim(numer_win, column, PATCH, 3)
            numer_win = lax.dynamic_update_slice_in_dim(numer_win, previous + weight * result, column, 3)
            previous_den = lax.dynamic_slice_in_dim(denom_win, column, PATCH, 1)
            denom_win = lax.dynamic_update_slice_in_dim(denom_win, previous_den + weight, column, 1)
        numer_all = lax.dynamic_update_slice_in_dim(numer_all, numer_win, row_start, 2)
        denom_all = lax.dynamic_update_slice_in_dim(denom_all, denom_win, row_start, 0)
        return ((numer_all, denom_all), 0)
    initial = (jnp.zeros((MEMBERS, CH, ROWS + PATCH, COLS), jnp.float32), jnp.zeros((ROWS + PATCH, COLS), jnp.float32))
    sums_out, unused_out = lax.scan(holder_step, initial, jnp.arange(N_TILE, dtype=jnp.int32))
    numer_dom = sums_out[0][:, :, :ROWS]
    denom_dom = sums_out[1][:ROWS]
    members = reg_mean[None] + numer_dom / jnp.maximum(denom_dom, 1.0)[None, None]
    ens_mean = lax.optimization_barrier(jnp.mean(members, axis=0))
    ens_var = lax.optimization_barrier(jnp.mean((members - ens_mean[None]) ** 2, axis=0))
    return (ens_mean, ens_var)
```

```python
import math

import jax
import jax.numpy as jnp
from jax import lax
from jax.experimental import pallas as pl
from jax.experimental.pallas import tpu as pltpu
from jax.sharding import PartitionSpec as P

POOL = 4


skip_gain = 0.2
out_gain = 0.5 / math.sqrt(1.25)
in_gain = 1.0 / math.sqrt(1.25)


def shifted(value, axis, steps):
    count = lax.axis_size(axis)
    initial, last = (max(0, -steps), min(count, count - steps))
    return lax.ppermute(value, axis, [(source, source + steps) for source in range(initial, last)])


def extended(cells, axis, dim, width):
    head = lax.slice_in_dim(cells, 0, width, axis=dim)
    tail = lax.slice_in_dim(cells, cells.shape[dim] - width, cells.shape[dim], axis=dim)
    return jnp.concatenate([shifted(tail, axis, 1), cells, shifted(head, axis, -1)], axis=dim)


def conv(cells, kernel, row_pad):
    feat_in, feat_out = kernel.shape[1:]
    return lax.conv_general_dilated(
        cells,
        kernel.reshape(3, 3, feat_in, feat_out),
        (1, 1),
        ((row_pad, row_pad), (1, 1)),
        dimension_numbers=("NHWC", "HWIO", "NHWC"),
        preferred_element_type=jnp.float32,
    )


def residual_layer(hidden_act, conv_term):
    return (hidden_act.astype(jnp.float32) + jax.nn.silu(conv_term)).astype(jnp.bfloat16)


def regress(coarse, regress_lift, regress_conv, regress_head):
    channel_count, row_total, col_total = coarse.shape
    block_rows, block_cols = row_total // POOL, col_total // POOL
    layer_count = regress_conv.shape[0]
    owner = jnp.arange(col_total)[:, None] // POOL == jnp.arange(block_cols)[None, :]
    col_sums = jnp.dot(
        coarse.reshape(-1, col_total), owner.astype(jnp.bfloat16), preferred_element_type=jnp.float32
    )
    sums = col_sums.reshape(channel_count, block_rows, POOL, block_cols).sum(axis=2)
    coarse_low = (sums * (1.0 / (POOL * POOL))).astype(jnp.bfloat16)
    rimmed = extended(coarse_low, "tile", 1, layer_count)
    hidden_act = jnp.einsum(
        "crw,ck->rwk", rimmed, regress_lift, preferred_element_type=jnp.float32
    ).astype(jnp.bfloat16)
    first_row = lax.axis_index("tile") * block_rows - layer_count
    domain_rows = lax.axis_size("tile") * block_rows
    for layer_index in range(layer_count):
        conv_term = conv(hidden_act[None], regress_conv[layer_index], 0)[0]
        hidden_act = residual_layer(hidden_act[1:-1], conv_term)
        first_row = first_row + 1
        rows = first_row + jnp.arange(hidden_act.shape[0])
        inside = jnp.logical_and(rows >= 0, rows < domain_rows)
        hidden_act = jnp.where(inside[:, None, None], hidden_act, jnp.zeros_like(hidden_act))
    reg_low = jnp.einsum(
        "rwk,kc->crw", hidden_act, regress_head, preferred_element_type=jnp.float32
    )
    wide = jnp.dot(
        reg_low.reshape(-1, block_cols),
        owner.T.astype(jnp.float32),
        precision=lax.Precision.HIGHEST,
        preferred_element_type=jnp.float32,
    ).reshape(channel_count, block_rows, 1, col_total)
    wide = jnp.broadcast_to(wide, (channel_count, block_rows, POOL, col_total))
    return coarse.astype(jnp.float32) + wide.reshape(coarse.shape)


def repeated(base, times):
    eye = jnp.eye(times, dtype=base.dtype)
    return (eye[:, None, :, None] * base[None, :, None, :]).reshape(
        times * base.shape[0], times * base.shape[1]
    )


def blend_kernel(slot_total, strip_rows, feat_rows, table_ref, heads_ref, weight_ref, acc_ref, den_ref):
    acc_ref[...] = jnp.zeros_like(acc_ref)
    den_ref[...] = jnp.zeros_like(den_ref)
    block_cols = heads_ref.shape[1]
    col_total = weight_ref.shape[1]

    def step(index, carry):
        offset = index // slot_total
        slot = index - offset * slot_total
        column = table_ref[offset * (slot_total + 1) + slot]
        live = slot < table_ref[offset * (slot_total + 1) + slot_total]

        @pl.when(live)
        def _():
            term = heads_ref[index]
            high = term.astype(jnp.bfloat16)
            low = (term - high.astype(jnp.float32)).astype(jnp.bfloat16)
            cols = lax.broadcasted_iota(jnp.int32, (block_cols, col_total), 1)
            blocks = lax.broadcasted_iota(jnp.int32, (block_cols, col_total), 0)
            pick = jnp.where(((cols - column) >> 2) == blocks, 1.0, 0.0).astype(jnp.bfloat16)
            dims = (((0,), (0,)), ((), ()))
            placed = lax.dot_general(
                high, pick, dims, preferred_element_type=jnp.float32
            ) + lax.dot_general(low, pick, dims, preferred_element_type=jnp.float32)
            start = pl.multiple_of(offset * strip_rows, strip_rows)
            weights = pltpu.roll(weight_ref[pl.ds(start, strip_rows), :], column, axis=1)
            den_ref[...] += weights
            for row in range(strip_rows):
                base = (row // POOL) * feat_rows
                acc_ref[row] += weights[row : row + 1, :] * placed[base : base + feat_rows, :]

        return carry

    lax.fori_loop(0, heads_ref.shape[0], step, 0)


def blend(table, heads, weights, slot_total, strip_rows, feat_rows):
    col_total = weights.shape[1]
    vmem = pl.BlockSpec(memory_space=pltpu.VMEM)
    return pl.pallas_call(
        lambda *refs: blend_kernel(slot_total, strip_rows, feat_rows, *refs),
        out_shape=(
            jax.ShapeDtypeStruct((strip_rows, feat_rows, col_total), jnp.float32),
            jax.ShapeDtypeStruct((strip_rows, col_total), jnp.float32),
        ),
        in_specs=[pl.BlockSpec(memory_space=pltpu.SMEM), vmem, vmem],
        out_specs=(vmem, vmem),
        name="blend",
    )(table, heads, weights)


def local(
    coarse,
    noise_field,
    anchors,
    counts,
    blend_weights,
    regress_lift,
    regress_conv,
    regress_head,
    denoise_lift,
    denoise_conv,
    denoise_head,
):
    members, channels, strip_rows, col_total = noise_field.shape
    patch_size = blend_weights.shape[0]
    width = denoise_lift.shape[1]
    span = patch_size // strip_rows
    slot_total = anchors.shape[1]
    block_rows = strip_rows // POOL
    block_cols = patch_size // POOL
    feat_rows = members * channels

    table = jnp.concatenate([anchors, counts[:, None]], axis=1)
    reach = 1
    while reach < span:
        table = jnp.concatenate([table, shifted(table, "tile", reach)], axis=0)
        reach *= 2
    table = table[:span]

    reg_mean = regress(coarse, regress_lift, regress_conv, regress_head)

    fields = jnp.concatenate(
        [noise_field.reshape(feat_rows, strip_rows, col_total), reg_mean.astype(jnp.bfloat16), coarse]
    )
    field_count = fields.shape[0]
    row_sums = (
        fields.astype(jnp.float32)
        .reshape(field_count, block_rows, POOL, col_total)
        .sum(axis=2)
        .transpose(1, 0, 2)
    )
    row_sums = jnp.pad(row_sums, ((0, 0), (0, 0), (0, POOL - 1)))
    sums = sum(row_sums[:, :, at : at + col_total] for at in range(POOL))
    low_all = (sums * (1.0 / (POOL * POOL))).astype(jnp.bfloat16).reshape(-1, col_total)
    starts = table[:, :slot_total, None] + POOL * jnp.arange(block_cols, dtype=jnp.int32)
    pick = (starts.reshape(-1, 1) == jnp.arange(col_total, dtype=jnp.int32)[None]).astype(jnp.bfloat16)
    cut = lax.dot_general(
        pick, low_all, (((1,), (1,)), ((), ())), preferred_element_type=jnp.float32
    )
    cut = cut.astype(jnp.bfloat16).reshape(span, slot_total, block_cols, block_rows * field_count)
    low = jnp.stack([cut[0]] + [shifted(cut[at], "tile", -at) for at in range(1, span)])
    low = low.reshape(-1, block_rows * field_count)

    noise_base = repeated(denoise_lift[:channels], members)
    noise_base = jnp.pad(noise_base, ((0, 2 * channels), (0, 0)))
    cond_base = jnp.tile(denoise_lift[channels:], (1, members))
    cond_base = jnp.pad(cond_base, ((feat_rows, 0), (0, 0)))
    lifted = in_gain * jnp.dot(
        low, repeated(noise_base, block_rows), preferred_element_type=jnp.float32
    ) + jnp.dot(low, repeated(cond_base, block_rows), preferred_element_type=jnp.float32)
    hidden_act = (
        lifted.astype(jnp.bfloat16)
        .reshape(span, slot_total, block_cols, block_rows, members, width)
        .transpose(1, 4, 0, 3, 2, 5)
        .reshape(slot_total * members, span * block_rows, block_cols, width)
    )
    for layer_index in range(denoise_conv.shape[0]):
        hidden_act = residual_layer(hidden_act, conv(hidden_act, denoise_conv[layer_index], 1))
    hidden_act = (
        hidden_act.reshape(slot_total, members, span, block_rows, block_cols, width)
        .transpose(2, 0, 4, 3, 1, 5)
        .reshape(span * slot_total * block_cols, block_rows * members * width)
    )
    head = repeated(denoise_head, block_rows * members)
    head = jnp.pad(head, ((0, 0), (0, -head.shape[1] % 128)))
    heads = jnp.dot(hidden_act, head, preferred_element_type=jnp.float32)
    heads = heads.reshape(span, slot_total, block_cols, head.shape[1])
    heads = jnp.stack([heads[0]] + [shifted(heads[at], "tile", at) for at in range(1, span)])

    weights = jnp.pad(blend_weights.astype(jnp.float32), ((0, 0), (0, col_total - patch_size)))
    acc, denom = blend(
        table.reshape(-1),
        heads.reshape(span * slot_total, block_cols, head.shape[1]),
        weights,
        slot_total,
        strip_rows,
        feat_rows,
    )
    acc = acc.reshape(strip_rows, members, channels, col_total).transpose(1, 2, 0, 3)
    numer = skip_gain * noise_field.astype(jnp.float32) * denom + out_gain * acc
    outs = reg_mean[None] + numer / jnp.maximum(denom, 1.0)
    ens_mean = jnp.mean(outs, axis=0)
    ens_var = jnp.mean((outs - ens_mean[None]) ** 2, axis=0)
    return (ens_mean, ens_var)


def solution(mesh):
    in_specs = (
        P(None, ("groups", "tile"), None),
        P(None, None, ("groups", "tile"), None),
        P(("groups", "tile"), None),
        P(("groups", "tile")),
        P(),
        P(),
        P(),
        P(),
        P(),
        P(),
        P(),
    )
    out_specs = (P(None, ("groups", "tile"), None), P(None, ("groups", "tile"), None))
    return jax.shard_map(local, mesh=mesh, in_specs=in_specs, out_specs=out_specs, check_vma=False)
```

```python
import math

import jax
import jax.numpy as jnp
from jax import lax
from jax.experimental import pallas as pl
from jax.experimental.pallas import tpu as pltpu
from jax.sharding import PartitionSpec as P

POOL = 4

skip_gain = 0.2
out_gain = 0.5 / math.sqrt(1.25)
in_gain = 1.0 / math.sqrt(1.25)


def exchange_kernel(moves, array_total, *refs):
    sources = refs[:array_total]
    targets = refs[array_total : 2 * array_total]
    send_sem, recv_sem = refs[2 * array_total :]
    mine = lax.axis_index("tile")
    count = lax.axis_size("tile")
    barrier = pltpu.get_barrier_semaphore()

    def holds(place):
        return jnp.logical_and(place >= 0, place < count)

    steps = sorted({move[3] for move in moves if move[3]})
    for step in steps:
        pl.semaphore_signal(
            barrier,
            inc=1,
            device_id={"tile": lax.rem(mine - step + count, count)},
            device_id_type=pl.DeviceIdType.MESH,
        )
    pl.semaphore_wait(barrier, len(steps))

    def copy_of(index):
        at, source, target, step = moves[index]
        return pltpu.make_async_remote_copy(
            src_ref=sources[at].at[source],
            dst_ref=targets[at].at[target],
            send_sem=send_sem.at[index],
            recv_sem=recv_sem.at[index],
            device_id={"tile": mine + step},
            device_id_type=pl.DeviceIdType.MESH,
        )

    for index, (at, source, target, step) in enumerate(moves):
        if step:

            @pl.when(holds(mine + step))
            def _():
                copy_of(index).start()

    for index, (at, source, target, step) in enumerate(moves):
        if step:

            @pl.when(jnp.logical_not(holds(mine - step)))
            def _():
                targets[at][target] = jnp.zeros(targets[at].shape[1:], targets[at].dtype)

        else:
            targets[at][target] = sources[at][source]
    for index, (at, source, target, step) in enumerate(moves):
        if step:

            @pl.when(holds(mine - step))
            def _():
                copy_of(index).wait_recv()

            @pl.when(holds(mine + step))
            def _():
                copy_of(index).wait_send()


def exchange(arrays, slots, moves, collective_id):
    vmem = pl.BlockSpec(memory_space=pltpu.VMEM)
    return pl.pallas_call(
        lambda *refs: exchange_kernel(moves, len(arrays), *refs),
        out_shape=tuple(
            jax.ShapeDtypeStruct((slot_count,) + array.shape[1:], array.dtype)
            for array, slot_count in zip(arrays, slots)
        ),
        in_specs=[vmem] * len(arrays),
        out_specs=(vmem,) * len(arrays),
        scratch_shapes=[
            pltpu.SemaphoreType.DMA((len(moves),)),
            pltpu.SemaphoreType.DMA((len(moves),)),
        ],
        compiler_params=pltpu.CompilerParams(collective_id=collective_id, has_side_effects=True),
        name="exchange%d" % collective_id,
    )(*arrays)


def conv(cells, kernel, row_pad):
    feat_in, feat_out = kernel.shape[1:]
    return lax.conv_general_dilated(
        cells,
        kernel.reshape(3, 3, feat_in, feat_out),
        (1, 1),
        ((row_pad, row_pad), (1, 1)),
        dimension_numbers=("NHWC", "HWIO", "NHWC"),
        preferred_element_type=jnp.float32,
    )


def residual_layer(hidden_act, conv_term):
    return (hidden_act.astype(jnp.float32) + jax.nn.silu(conv_term)).astype(jnp.bfloat16)


def regress(coarse, table, span, regress_lift, regress_conv, regress_head):
    channel_count, row_total, col_total = coarse.shape
    block_rows, block_cols = row_total // POOL, col_total // POOL
    layer_count = regress_conv.shape[0]
    owner = jnp.arange(col_total)[:, None] // POOL == jnp.arange(block_cols)[None, :]
    col_sums = jnp.dot(
        coarse.reshape(-1, col_total), owner.astype(jnp.bfloat16), preferred_element_type=jnp.float32
    )
    sums = col_sums.reshape(channel_count, block_rows, POOL, block_cols).sum(axis=2)
    coarse_low = (sums * (1.0 / (POOL * POOL))).astype(jnp.bfloat16)
    rows_first = coarse_low.transpose(1, 0, 2)
    rims = jnp.stack([rows_first[block_rows - layer_count :], rows_first[:layer_count]])
    moves = [(0, 0, at, at) for at in range(span - 1, -1, -1)] + [(1, 0, 0, 1), (1, 1, 1, -1)]
    tables, rims = exchange(
        (table[None], rims.reshape(2, layer_count * channel_count, block_cols)), (span, 2), moves, 0
    )
    rims = rims.reshape(2, layer_count, channel_count, block_cols)
    rimmed = jnp.concatenate([rims[0], rows_first, rims[1]]).transpose(1, 0, 2)
    hidden_act = jnp.einsum(
        "crw,ck->rwk", rimmed, regress_lift, preferred_element_type=jnp.float32
    ).astype(jnp.bfloat16)
    first_row = lax.axis_index("tile") * block_rows - layer_count
    domain_rows = lax.axis_size("tile") * block_rows
    for layer_index in range(layer_count):
        conv_term = conv(hidden_act[None], regress_conv[layer_index], 0)[0]
        hidden_act = residual_layer(hidden_act[1:-1], conv_term)
        first_row = first_row + 1
        rows = first_row + jnp.arange(hidden_act.shape[0])
        inside = jnp.logical_and(rows >= 0, rows < domain_rows)
        hidden_act = jnp.where(inside[:, None, None], hidden_act, jnp.zeros_like(hidden_act))
    reg_low = jnp.einsum(
        "rwk,kc->crw", hidden_act, regress_head, preferred_element_type=jnp.float32
    )
    wide = jnp.dot(
        reg_low.reshape(-1, block_cols),
        owner.T.astype(jnp.float32),
        precision=lax.Precision.HIGHEST,
        preferred_element_type=jnp.float32,
    ).reshape(channel_count, block_rows, 1, col_total)
    wide = jnp.broadcast_to(wide, (channel_count, block_rows, POOL, col_total))
    return coarse.astype(jnp.float32) + wide.reshape(coarse.shape), tables


def repeated(base, times):
    eye = jnp.eye(times, dtype=base.dtype)
    return (eye[:, None, :, None] * base[None, :, None, :]).reshape(
        times * base.shape[0], times * base.shape[1]
    )


def blend_kernel(slot_total, strip_rows, feat_rows, table_ref, heads_ref, weight_ref, acc_ref, den_ref):
    acc_ref[...] = jnp.zeros_like(acc_ref)
    den_ref[...] = jnp.zeros_like(den_ref)
    block_cols = heads_ref.shape[1]
    col_total = weight_ref.shape[1]

    def step(index, carry):
        offset = index // slot_total
        slot = index - offset * slot_total
        column = table_ref[offset * (slot_total + 1) + slot]
        live = slot < table_ref[offset * (slot_total + 1) + slot_total]

        @pl.when(live)
        def _():
            term = heads_ref[index]
            high = term.astype(jnp.bfloat16)
            low = (term - high.astype(jnp.float32)).astype(jnp.bfloat16)
            cols = lax.broadcasted_iota(jnp.int32, (block_cols, col_total), 1)
            blocks = lax.broadcasted_iota(jnp.int32, (block_cols, col_total), 0)
            pick = jnp.where(((cols - column) >> 2) == blocks, 1.0, 0.0).astype(jnp.bfloat16)
            dims = (((0,), (0,)), ((), ()))
            placed = lax.dot_general(
                high, pick, dims, preferred_element_type=jnp.float32
            ) + lax.dot_general(low, pick, dims, preferred_element_type=jnp.float32)
            start = pl.multiple_of(offset * strip_rows, strip_rows)
            weights = pltpu.roll(weight_ref[pl.ds(start, strip_rows), :], column, axis=1)
            den_ref[...] += weights
            for row in range(strip_rows):
                base = (row // POOL) * feat_rows
                acc_ref[row] += weights[row : row + 1, :] * placed[base : base + feat_rows, :]

        return carry

    lax.fori_loop(0, heads_ref.shape[0], step, 0)


def blend(table, heads, weights, slot_total, strip_rows, feat_rows):
    col_total = weights.shape[1]
    vmem = pl.BlockSpec(memory_space=pltpu.VMEM)
    return pl.pallas_call(
        lambda *refs: blend_kernel(slot_total, strip_rows, feat_rows, *refs),
        out_shape=(
            jax.ShapeDtypeStruct((strip_rows, feat_rows, col_total), jnp.float32),
            jax.ShapeDtypeStruct((strip_rows, col_total), jnp.float32),
        ),
        in_specs=[pl.BlockSpec(memory_space=pltpu.SMEM), vmem, vmem],
        out_specs=(vmem, vmem),
        name="blend",
    )(table, heads, weights)


def local(
    coarse,
    noise_field,
    anchors,
    counts,
    blend_weights,
    regress_lift,
    regress_conv,
    regress_head,
    denoise_lift,
    denoise_conv,
    denoise_head,
):
    members, channels, strip_rows, col_total = noise_field.shape
    patch_size = blend_weights.shape[0]
    width = denoise_lift.shape[1]
    span = patch_size // strip_rows
    slot_total = anchors.shape[1]
    block_rows = strip_rows // POOL
    block_cols = patch_size // POOL
    feat_rows = members * channels

    table = jnp.concatenate([anchors, counts[:, None]], axis=1)
    table = jnp.pad(table, ((0, 7), (0, 127 - slot_total)))
    reg_mean, tables = regress(coarse, table, span, regress_lift, regress_conv, regress_head)
    table = tables[:, 0, : slot_total + 1]

    fields = jnp.concatenate(
        [noise_field.reshape(feat_rows, strip_rows, col_total), reg_mean.astype(jnp.bfloat16), coarse]
    )
    field_count = fields.shape[0]
    row_sums = (
        fields.astype(jnp.float32)
        .reshape(field_count, block_rows, POOL, col_total)
        .sum(axis=2)
        .transpose(1, 0, 2)
    )
    row_sums = jnp.pad(row_sums, ((0, 0), (0, 0), (0, POOL - 1)))
    sums = sum(row_sums[:, :, at : at + col_total] for at in range(POOL))
    low_all = (sums * (1.0 / (POOL * POOL))).astype(jnp.bfloat16).reshape(-1, col_total)
    starts = table[:, :slot_total, None] + POOL * jnp.arange(block_cols, dtype=jnp.int32)
    pick = (starts.reshape(-1, 1) == jnp.arange(col_total, dtype=jnp.int32)[None]).astype(jnp.bfloat16)
    cut = lax.dot_general(
        pick, low_all, (((1,), (1,)), ((), ())), preferred_element_type=jnp.float32
    )
    cut = cut.astype(jnp.bfloat16).reshape(span, slot_total * block_cols, block_rows * field_count)
    farthest = range(span - 1, -1, -1)
    (low,) = exchange((cut,), (span,), [(0, at, at, -at) for at in farthest], 1)
    low = low.reshape(-1, block_rows * field_count)

    noise_base = repeated(denoise_lift[:channels], members)
    noise_base = jnp.pad(noise_base, ((0, 2 * channels), (0, 0)))
    cond_base = jnp.tile(denoise_lift[channels:], (1, members))
    cond_base = jnp.pad(cond_base, ((feat_rows, 0), (0, 0)))
    lifted = in_gain * jnp.dot(
        low, repeated(noise_base, block_rows), preferred_element_type=jnp.float32
    ) + jnp.dot(low, repeated(cond_base, block_rows), preferred_element_type=jnp.float32)
    hidden_act = (
        lifted.astype(jnp.bfloat16)
        .reshape(span, slot_total, block_cols, block_rows, members, width)
        .transpose(1, 4, 0, 3, 2, 5)
        .reshape(slot_total * members, span * block_rows, block_cols, width)
    )
    for layer_index in range(denoise_conv.shape[0]):
        hidden_act = residual_layer(hidden_act, conv(hidden_act, denoise_conv[layer_index], 1))
    hidden_act = (
        hidden_act.reshape(slot_total, members, span, block_rows, block_cols, width)
        .transpose(2, 0, 4, 3, 1, 5)
        .reshape(span * slot_total * block_cols, block_rows * members * width)
    )
    head = repeated(denoise_head, block_rows * members)
    head = jnp.pad(head, ((0, 0), (0, -head.shape[1] % 128)))
    heads = jnp.dot(hidden_act, head, preferred_element_type=jnp.float32)
    heads = heads.reshape(span, slot_total * block_cols, head.shape[1])
    (heads,) = exchange((heads,), (span,), [(0, at, at, at) for at in farthest], 2)

    weights = jnp.pad(blend_weights.astype(jnp.float32), ((0, 0), (0, col_total - patch_size)))
    acc, denom = blend(
        table.reshape(-1),
        heads.reshape(span * slot_total, block_cols, head.shape[1]),
        weights,
        slot_total,
        strip_rows,
        feat_rows,
    )
    acc = acc.reshape(strip_rows, members, channels, col_total).transpose(1, 2, 0, 3)
    numer = skip_gain * noise_field.astype(jnp.float32) * denom + out_gain * acc
    outs = reg_mean[None] + numer / jnp.maximum(denom, 1.0)
    ens_mean = jnp.mean(outs, axis=0)
    ens_var = jnp.mean((outs - ens_mean[None]) ** 2, axis=0)
    return (ens_mean, ens_var)


def solution(mesh):
    in_specs = (
        P(None, ("groups", "tile"), None),
        P(None, None, ("groups", "tile"), None),
        P(("groups", "tile"), None),
        P(("groups", "tile")),
        P(),
        P(),
        P(),
        P(),
        P(),
        P(),
        P(),
    )
    out_specs = (P(None, ("groups", "tile"), None), P(None, ("groups", "tile"), None))
    return jax.shard_map(local, mesh=mesh, in_specs=in_specs, out_specs=out_specs, check_vma=False)
```

```python
import math

import jax
import jax.numpy as jnp
from jax import lax
from jax.experimental import pallas as pl
from jax.experimental.pallas import tpu as pltpu
from jax.sharding import PartitionSpec as P

POOL = 4

skip_gain = 0.2
out_gain = 0.5 / math.sqrt(1.25)
in_gain = 1.0 / math.sqrt(1.25)


def exchange_kernel(moves, array_total, *refs):
    sources = refs[:array_total]
    targets = refs[array_total : 2 * array_total]
    send_sem, recv_sem = refs[2 * array_total :]
    mine = lax.axis_index("tile")
    count = lax.axis_size("tile")
    barrier = pltpu.get_barrier_semaphore()

    def holds(place):
        return jnp.logical_and(place >= 0, place < count)

    steps = sorted({move[3] for move in moves if move[3]})
    for step in steps:
        pl.semaphore_signal(
            barrier,
            inc=1,
            device_id={"tile": lax.rem(mine - step + count, count)},
            device_id_type=pl.DeviceIdType.MESH,
        )
    pl.semaphore_wait(barrier, len(steps))

    def copy_of(index):
        at, source, target, step = moves[index]
        return pltpu.make_async_remote_copy(
            src_ref=sources[at].at[source],
            dst_ref=targets[at].at[target],
            send_sem=send_sem.at[index],
            recv_sem=recv_sem.at[index],
            device_id={"tile": mine + step},
            device_id_type=pl.DeviceIdType.MESH,
        )

    for index, (at, source, target, step) in enumerate(moves):
        if step:

            @pl.when(holds(mine + step))
            def _():
                copy_of(index).start()

    for index, (at, source, target, step) in enumerate(moves):
        if step:

            @pl.when(jnp.logical_not(holds(mine - step)))
            def _():
                targets[at][target] = jnp.zeros(targets[at].shape[1:], targets[at].dtype)

        else:
            targets[at][target] = sources[at][source]
    for index, (at, source, target, step) in enumerate(moves):
        if step:

            @pl.when(holds(mine - step))
            def _():
                copy_of(index).wait_recv()

            @pl.when(holds(mine + step))
            def _():
                copy_of(index).wait_send()


def exchange(arrays, slots, moves, collective_id):
    vmem = pl.BlockSpec(memory_space=pltpu.VMEM)
    return pl.pallas_call(
        lambda *refs: exchange_kernel(moves, len(arrays), *refs),
        out_shape=tuple(
            jax.ShapeDtypeStruct((slot_count,) + array.shape[1:], array.dtype)
            for array, slot_count in zip(arrays, slots)
        ),
        in_specs=[vmem] * len(arrays),
        out_specs=(vmem,) * len(arrays),
        scratch_shapes=[
            pltpu.SemaphoreType.DMA((len(moves),)),
            pltpu.SemaphoreType.DMA((len(moves),)),
        ],
        compiler_params=pltpu.CompilerParams(collective_id=collective_id, has_side_effects=True),
        name="exchange%d" % collective_id,
    )(*arrays)


def conv(cells, kernel, row_pad):
    feat_in, feat_out = kernel.shape[1:]
    return lax.conv_general_dilated(
        cells,
        kernel.reshape(3, 3, feat_in, feat_out),
        (1, 1),
        ((row_pad, row_pad), (1, 1)),
        dimension_numbers=("NHWC", "HWIO", "NHWC"),
        preferred_element_type=jnp.float32,
    )


def residual_layer(hidden_act, conv_term):
    return (hidden_act.astype(jnp.float32) + jax.nn.silu(conv_term)).astype(jnp.bfloat16)


def regress(coarse, table, span, regress_lift, regress_conv, regress_head):
    channel_count, row_total, col_total = coarse.shape
    block_rows, block_cols = row_total // POOL, col_total // POOL
    layer_count = regress_conv.shape[0]
    owner = jnp.arange(col_total)[:, None] // POOL == jnp.arange(block_cols)[None, :]
    col_sums = jnp.dot(
        coarse.reshape(-1, col_total), owner.astype(jnp.bfloat16), preferred_element_type=jnp.float32
    )
    sums = col_sums.reshape(channel_count, block_rows, POOL, block_cols).sum(axis=2)
    coarse_low = (sums * (1.0 / (POOL * POOL))).astype(jnp.bfloat16)
    rows_first = coarse_low.transpose(1, 0, 2)
    rims = jnp.stack([rows_first[block_rows - layer_count :], rows_first[:layer_count]])
    moves = [(0, 0, at, at) for at in range(span - 1, -1, -1)] + [(1, 0, 0, 1), (1, 1, 1, -1)]
    tables, rims = exchange(
        (table[None], rims.reshape(2, layer_count * channel_count, block_cols)), (span, 2), moves, 0
    )
    rims = rims.reshape(2, layer_count, channel_count, block_cols)
    rimmed = jnp.concatenate([rims[0], rows_first, rims[1]]).transpose(1, 0, 2)
    hidden_act = jnp.einsum(
        "crw,ck->rwk", rimmed, regress_lift, preferred_element_type=jnp.float32
    ).astype(jnp.bfloat16)
    first_row = lax.axis_index("tile") * block_rows - layer_count
    domain_rows = lax.axis_size("tile") * block_rows
    for layer_index in range(layer_count):
        conv_term = conv(hidden_act[None], regress_conv[layer_index], 0)[0]
        hidden_act = residual_layer(hidden_act[1:-1], conv_term)
        first_row = first_row + 1
        rows = first_row + jnp.arange(hidden_act.shape[0])
        inside = jnp.logical_and(rows >= 0, rows < domain_rows)
        hidden_act = jnp.where(inside[:, None, None], hidden_act, jnp.zeros_like(hidden_act))
    reg_low = jnp.einsum(
        "rwk,kc->crw", hidden_act, regress_head, preferred_element_type=jnp.float32
    )
    wide = jnp.dot(
        reg_low.reshape(-1, block_cols),
        owner.T.astype(jnp.float32),
        precision=lax.Precision.HIGHEST,
        preferred_element_type=jnp.float32,
    ).reshape(channel_count, block_rows, 1, col_total)
    wide = jnp.broadcast_to(wide, (channel_count, block_rows, POOL, col_total))
    return coarse.astype(jnp.float32) + wide.reshape(coarse.shape), tables


def repeated(base, times):
    eye = jnp.eye(times, dtype=base.dtype)
    return (eye[:, None, :, None] * base[None, :, None, :]).reshape(
        times * base.shape[0], times * base.shape[1]
    )


def blend_kernel(slot_total, strip_rows, feat_rows, table_ref, heads_ref, weight_ref, acc_ref, den_ref):
    acc_ref[...] = jnp.zeros_like(acc_ref)
    den_ref[...] = jnp.zeros_like(den_ref)
    block_cols = heads_ref.shape[1]
    col_total = weight_ref.shape[1]

    def step(index, carry):
        offset = index // slot_total
        slot = index - offset * slot_total
        column = table_ref[offset * (slot_total + 1) + slot]
        live = slot < table_ref[offset * (slot_total + 1) + slot_total]

        @pl.when(live)
        def _():
            term = heads_ref[index]
            high = term.astype(jnp.bfloat16)
            low = (term - high.astype(jnp.float32)).astype(jnp.bfloat16)
            cols = lax.broadcasted_iota(jnp.int32, (block_cols, col_total), 1)
            blocks = lax.broadcasted_iota(jnp.int32, (block_cols, col_total), 0)
            pick = jnp.where(((cols - column) >> 2) == blocks, 1.0, 0.0).astype(jnp.bfloat16)
            dims = (((0,), (0,)), ((), ()))
            placed = lax.dot_general(
                high, pick, dims, preferred_element_type=jnp.float32
            ) + lax.dot_general(low, pick, dims, preferred_element_type=jnp.float32)
            start = pl.multiple_of(offset * strip_rows, strip_rows)
            weights = pltpu.roll(weight_ref[pl.ds(start, strip_rows), :], column, axis=1)
            den_ref[...] += weights
            for row in range(strip_rows):
                base = (row // POOL) * feat_rows
                acc_ref[row] += weights[row : row + 1, :] * placed[base : base + feat_rows, :]

        return carry

    lax.fori_loop(0, heads_ref.shape[0], step, 0)


def blend(table, heads, weights, slot_total, strip_rows, feat_rows):
    col_total = weights.shape[1]
    vmem = pl.BlockSpec(memory_space=pltpu.VMEM)
    return pl.pallas_call(
        lambda *refs: blend_kernel(slot_total, strip_rows, feat_rows, *refs),
        out_shape=(
            jax.ShapeDtypeStruct((strip_rows, feat_rows, col_total), jnp.float32),
            jax.ShapeDtypeStruct((strip_rows, col_total), jnp.float32),
        ),
        in_specs=[pl.BlockSpec(memory_space=pltpu.SMEM), vmem, vmem],
        out_specs=(vmem, vmem),
        name="blend",
    )(table, heads, weights)


def local(
    coarse,
    noise_field,
    anchors,
    counts,
    blend_weights,
    regress_lift,
    regress_conv,
    regress_head,
    denoise_lift,
    denoise_conv,
    denoise_head,
):
    members, channels, strip_rows, col_total = noise_field.shape
    patch_size = blend_weights.shape[0]
    width = denoise_lift.shape[1]
    span = patch_size // strip_rows
    slot_total = anchors.shape[1]
    block_rows = strip_rows // POOL
    block_cols = patch_size // POOL
    feat_rows = members * channels

    table = jnp.concatenate([anchors, counts[:, None]], axis=1)
    table = jnp.pad(table, ((0, 7), (0, 127 - slot_total)))
    reg_mean, tables = regress(coarse, table, span, regress_lift, regress_conv, regress_head)
    table = tables[:, 0, : slot_total + 1]

    fields = jnp.concatenate(
        [noise_field.reshape(feat_rows, strip_rows, col_total), reg_mean.astype(jnp.bfloat16), coarse]
    )
    field_count = fields.shape[0]
    row_sums = (
        fields.astype(jnp.float32)
        .reshape(field_count, block_rows, POOL, col_total)
        .sum(axis=2)
        .transpose(1, 0, 2)
    )
    row_sums = jnp.pad(row_sums, ((0, 0), (0, 0), (0, POOL - 1)))
    sums = sum(row_sums[:, :, at : at + col_total] for at in range(POOL))
    low_all = (sums * (1.0 / (POOL * POOL))).astype(jnp.bfloat16).reshape(-1, col_total)
    starts = table[:, :slot_total, None] + POOL * jnp.arange(block_cols, dtype=jnp.int32)
    pick = (starts.reshape(-1, 1) == jnp.arange(col_total, dtype=jnp.int32)[None]).astype(jnp.bfloat16)
    cut = lax.dot_general(
        pick, low_all, (((1,), (1,)), ((), ())), preferred_element_type=jnp.float32
    )
    cut = cut.astype(jnp.bfloat16).reshape(span, slot_total * block_cols, block_rows * field_count)
    farthest = range(span - 1, -1, -1)
    half = slot_total * block_cols // 2
    tail = jnp.concatenate([cut[:, :half, 128:], cut[:, half:, 128:]], axis=2)
    cut = jnp.concatenate([cut[:, :, :128], tail], axis=1)
    (low,) = exchange((cut,), (span,), [(0, at, at, -at) for at in farthest], 1)
    side = (cut.shape[2] // 2) if half else 0
    tail = low[:, 2 * half :]
    tail = jnp.concatenate([tail[:, :, :side], tail[:, :, side:]], axis=1)
    low = jnp.concatenate([low[:, : 2 * half], tail], axis=2)
    low = low.reshape(-1, block_rows * field_count)

    noise_base = repeated(denoise_lift[:channels], members)
    noise_base = jnp.pad(noise_base, ((0, 2 * channels), (0, 0)))
    cond_base = jnp.tile(denoise_lift[channels:], (1, members))
    cond_base = jnp.pad(cond_base, ((feat_rows, 0), (0, 0)))
    lifted = in_gain * jnp.dot(
        low, repeated(noise_base, block_rows), preferred_element_type=jnp.float32
    ) + jnp.dot(low, repeated(cond_base, block_rows), preferred_element_type=jnp.float32)
    hidden_act = (
        lifted.astype(jnp.bfloat16)
        .reshape(span, slot_total, block_cols, block_rows, members, width)
        .transpose(1, 4, 0, 3, 2, 5)
        .reshape(slot_total * members, span * block_rows, block_cols, width)
    )
    for layer_index in range(denoise_conv.shape[0]):
        hidden_act = residual_layer(hidden_act, conv(hidden_act, denoise_conv[layer_index], 1))
    hidden_act = (
        hidden_act.reshape(slot_total, members, span, block_rows, block_cols, width)
        .transpose(2, 0, 4, 3, 1, 5)
        .reshape(span * slot_total * block_cols, block_rows * members * width)
    )
    head = repeated(denoise_head, block_rows * members)
    head_lanes = head.shape[1]
    spare = -head_lanes % 128
    head = jnp.pad(head, ((0, 0), (0, spare)))
    heads = jnp.dot(hidden_act, head, preferred_element_type=jnp.float32)
    heads = heads.reshape(span, slot_total * block_cols, head.shape[1])
    chunks = head_lanes // spare
    lot = heads.shape[1] // (chunks + 1)
    last = heads[:, chunks * lot :]
    side = jnp.concatenate([last[:, :, at * spare : (at + 1) * spare] for at in range(chunks)], axis=1)
    heads = jnp.concatenate([heads[:, : chunks * lot, :head_lanes], side], axis=2)
    (heads,) = exchange((heads,), (span,), [(0, at, at, at) for at in farthest], 2)
    last = [heads[:, at * lot : (at + 1) * lot, head_lanes:] for at in range(chunks)]
    last = jnp.concatenate(last, axis=2)
    heads = jnp.concatenate([heads[:, :, :head_lanes], last], axis=1)
    heads = jnp.pad(heads, ((0, 0), (0, 0), (0, spare)))

    weights = jnp.pad(blend_weights.astype(jnp.float32), ((0, 0), (0, col_total - patch_size)))
    acc, denom = blend(
        table.reshape(-1),
        heads.reshape(span * slot_total, block_cols, head.shape[1]),
        weights,
        slot_total,
        strip_rows,
        feat_rows,
    )
    acc = acc.reshape(strip_rows, members, channels, col_total).transpose(1, 2, 0, 3)
    numer = skip_gain * noise_field.astype(jnp.float32) * denom + out_gain * acc
    outs = reg_mean[None] + numer / jnp.maximum(denom, 1.0)
    ens_mean = jnp.mean(outs, axis=0)
    ens_var = jnp.mean((outs - ens_mean[None]) ** 2, axis=0)
    return (ens_mean, ens_var)


def solution(mesh):
    in_specs = (
        P(None, ("groups", "tile"), None),
        P(None, None, ("groups", "tile"), None),
        P(("groups", "tile"), None),
        P(("groups", "tile")),
        P(),
        P(),
        P(),
        P(),
        P(),
        P(),
        P(),
    )
    out_specs = (P(None, ("groups", "tile"), None), P(None, ("groups", "tile"), None))
    return jax.shard_map(local, mesh=mesh, in_specs=in_specs, out_specs=out_specs, check_vma=False)
```
